32 devices in a mesh: row: 8 (over y, x, core), col: 4 (over z).
Axes of the slice: x: 2, y: 2, z: 4, core: 2. Of those that a mesh axis runs over, the one named last changes fastest.
Arguments:
- coarse_feats: bfloat16 [64, 512], P(None, ('row', 'col')), may hold values from -6 to 6
- fine_feats: bfloat16 [64, 512], P(None, ('row', 'col')), may hold values from -6 to 6
- pair_prior: bfloat16 [64, 512, 512], P(None, 'row', 'col'), may hold values from -6 to 6
- zoom_start: int32 [2], replicated, may hold values from 0 to 256, as said below
- coarse_weights: bfloat16 [2, 3, 64, 192], replicated, may hold values from -0.25 to 0.25
- coarse_bias: float32 [2, 64], replicated, may hold values from -2.5 to 2.5
- refine_first: bfloat16 [3, 64, 384], replicated, may hold values from -0.1875 to 0.1875
- refine_second: bfloat16 [3, 64, 192], replicated, may hold values from -0.25 to 0.25
- refine_bias: float32 [2, 64], replicated, may hold values from -2.5 to 2.5
Outputs:
- coarse_map: bfloat16 [64, 512, 512], P(None, 'row', 'col')
- refined: bfloat16 [64, 512, 512], P(None, 'row', 'col')
The draws below stay inside these ranges and needn't reach their ends.
Inputs may be any that keep to these rules, and one draw needn't show every extreme that they name: `zoom_start`: the two entries are 0 and 256 in either order.
All inputs are finite; a program needn't handle non-finite values.
Results may differ from the reference program's by a relative error of at most 0.0059.
Values may be sent and summed in bfloat16 or wider, within the bound.
No kernel may reach another device: no remote copies, remote signals or barrier semaphores. Data moves between devices by JAX's collectives and lax.ppermute only.
A program may use at most 64 MiB of HBM per device.

```python
import jax
import jax.numpy as jnp
from jax import lax

C = 64
BINS = 512


def draw_zoom_start(key, part):
    picked = jax.random.randint(key, (1,), 0, 2)
    both = jnp.concatenate([picked, 1 - picked])
    return (both * (BINS // 2)).astype(jnp.int32)


def block_levels(stream_key, extent, shards, low, largest):
    loudness, own = 1.0, jax.random.fold_in(stream_key, 6)
    for position, parts in shards:
        draws = jnp.exp(jax.random.uniform(jax.random.fold_in(own, position), (parts,), jnp.float32, low / len(shards), largest / len(shards)))
        loudness = loudness * jnp.repeat(draws, extent[position] // parts).reshape([-1 if axis == position else 1 for axis in range(len(extent))])
    return loudness


def centred(own_key, shape, deviation, most, split=(), kind=jnp.bfloat16):
    values = jax.random.normal(own_key, shape, jnp.float32) * deviation
    if len(split) > 0:
        values = block_levels(own_key, shape, split, -0.22, 0.18) * values
    return jnp.clip(values, min=-most, max=most).astype(kind)


def setup_inputs(seed: int = 0) -> dict:
    arg_keys = jax.random.split(jax.random.key(seed), 10)
    return {
        "coarse_feats": centred(arg_keys[0], (C, BINS), 1.0, 6.0, ((1, 32),)),
        "fine_feats": centred(arg_keys[1], (C, BINS), 1.0, 6.0, ((1, 32),)),
        "pair_prior": centred(arg_keys[2], (C, BINS, BINS), 1.0, 6.0, ((1, 8), (2, 4))),
        "zoom_start": draw_zoom_start(jax.random.fold_in(arg_keys[9], 71), 0),
        "coarse_weights": centred(arg_keys[4], (2, 3, C, 3 * C), (9 * C) ** -0.5, 0.25),
        "coarse_bias": centred(arg_keys[5], (2, C), 0.5, 2.5, (), jnp.float32),
        "refine_first": centred(arg_keys[6], (3, C, 6 * C), (18 * C) ** -0.5, 0.1875),
        "refine_second": centred(arg_keys[7], (3, C, 3 * C), (9 * C) ** -0.5, 0.25),
        "refine_bias": centred(arg_keys[8], (2, C), 0.5, 2.5, (), jnp.float32),
    }


def conv_layer(source, weights, biases, spacing):
    inputs = source.shape[0]
    outputs = weights.shape[1]
    kernel = weights.astype(jnp.float32).reshape(3, outputs, 3, inputs).transpose(1, 3, 0, 2)
    result = lax.conv_general_dilated(
        source.astype(jnp.float32)[None], kernel, (1, 1),
        [(spacing, spacing), (spacing, spacing)], rhs_dilation=(spacing, spacing),
        dimension_numbers=("NCHW", "OIHW", "NCHW"))[0]
    return jnp.maximum(result + biases.astype(jnp.float32)[:, None, None], 0.0).astype(jnp.bfloat16)


def reference(coarse_feats, fine_feats, pair_prior, zoom_start, coarse_weights, coarse_bias, refine_first, refine_second, refine_bias):
    coarse_wide = coarse_feats.astype(jnp.float32)
    pair_map = (coarse_wide[:, :, None] + coarse_wide[:, None, :] + pair_prior.astype(jnp.float32)).astype(jnp.bfloat16)
    hidden_coarse = conv_layer(pair_map, coarse_weights[0], coarse_bias[0], 2)
    coarse_map = conv_layer(hidden_coarse, coarse_weights[1], coarse_bias[1], 4)
    zoom_bin = zoom_start[0].astype(jnp.int32)
    window = lax.dynamic_slice(coarse_map, (jnp.int32(0), zoom_bin, zoom_bin), (C, BINS // 2, BINS // 2))
    window = jnp.repeat(jnp.repeat(window, 2, axis=1), 2, axis=2)
    fine_wide = fine_feats.astype(jnp.float32)
    fine_pair = (fine_wide[:, :, None] + fine_wide[:, None, :]).astype(jnp.bfloat16)
    joined = jnp.concatenate([window, fine_pair], axis=0)
    hidden_refine = conv_layer(joined, refine_first, refine_bias[0], 8)
    refined = conv_layer(hidden_refine, refine_second, refine_bias[1], 16)
    return coarse_map, refined
```

```python
import jax
import jax.numpy as jnp
from jax import lax
from jax.experimental import pallas as pl
from jax.experimental.pallas import tpu as pltpu
from jax.sharding import PartitionSpec as P

f32 = jnp.float32
bf16 = jnp.bfloat16
VMEM = pl.BlockSpec(memory_space=pltpu.VMEM)
SMEM = pl.BlockSpec(memory_space=pltpu.SMEM)


def call(body, outs, scratch, cost, name):
    flops, moved = cost
    def run(*args):
        return pl.pallas_call(
            body,
            out_shape=outs,
            in_specs=[SMEM] + [VMEM] * (len(args) - 1),
            out_specs=jax.tree.map(lambda _: VMEM, outs),
            scratch_shapes=scratch,
            compiler_params=pltpu.CompilerParams(vmem_limit_bytes=56 << 20),
            cost_estimate=pl.CostEstimate(flops=flops, bytes_accessed=moved, transcendentals=0),
            name=name,
        )(*args)

    return run


def roll(x, shift):
    shift = shift % x.shape[-1]
    return x if shift == 0 else pltpu.roll(x, shift, x.ndim - 1)


def lanes(shape):
    return lax.broadcasted_iota(jnp.int32, shape, len(shape) - 1)


def swap_pairs(count):
    first = [(i, i ^ 1) for i in range(count)]
    second = [(i, i + 1) for i in range(1, count - 1, 2)]
    return first, second + [(b, a) for a, b in second]


def dot(a, b):
    return jnp.dot(a, b, preferred_element_type=f32)


def pick_bins(feats, start, step):
    bins = feats.shape[0]
    shape = (bins, 128)
    hit = lax.broadcasted_iota(jnp.int32, shape, 0) == start + step * lanes(shape)
    return lax.dot_general(
        feats, hit.astype(f32).astype(bf16), (((0,), (0,)), ((), ())), preferred_element_type=f32
    )


def inside(start, step, bins, shape=(1, 128)):
    at = start + step * lanes(shape)
    return ((at >= 0) & (at < bins)).astype(f32)


def scalar_inside(at, bins):
    return ((at >= 0) & (at < bins)).astype(f32)


def strip_pack_tile(pos, center, row_a, row_b, out_a, out_b):
    rim = row_a.shape[0]
    rows = center.shape[0]
    odd_row = pos[0] % 2 == 1
    odd_col = pos[1] % 2 == 1
    lane = lanes(row_a.shape[1:]) // 8
    total = rows + 2 * rim
    for group in range(out_a.shape[0]):
        packed_a = jnp.zeros(row_a.shape[1:], f32)
        packed_b = packed_a
        for k in range(16):
            e = group * 16 + k
            if e >= total:
                break
            if e < rim:
                x = jnp.where(odd_row, row_a[e], row_b[e])
            elif e < rim + rows:
                x = center[e - rim]
            else:
                x = jnp.where(odd_row, row_b[e - rim - rows], row_a[e - rim - rows])
            x = x.astype(f32)
            turned = roll(x, 8)
            here = lane == k
            packed_a = jnp.where(here, roll(jnp.where(odd_col, x, turned), 8 * k), packed_a)
            packed_b = jnp.where(here, roll(jnp.where(odd_col, turned, x), 8 * k), packed_b)
        out_a[group] = packed_a.astype(bf16)
        out_b[group] = packed_b.astype(bf16)


def store_taps(ref, row, first, value, spacing):
    size = value.shape[0]
    for tap in range(3):
        ref[row, tap * size : (tap + 1) * size, first : first + 128] = roll(
            value, -spacing * tap
        ).astype(bf16)


def products(weights, taps, out, count):
    def one(row, carry):
        out[row] = dot(weights, taps[row])
        return carry

    lax.fori_loop(0, count, one, 0, unroll=4)


def combine(parts, row, spacing):
    size = parts.shape[1] // 3
    return (
        parts[row, :size]
        + parts[row + spacing, size : 2 * size]
        + parts[row + 2 * spacing, 2 * size :]
    )


def tile_kernel(
    pos, weights, bias, feats, center, row_a, row_b, col_a, col_b,
    coarse, m00, m01, m10, m11, s1, s2, parts, own_feats,
):
    rows, channels, width = center.shape
    half = width // 2
    rim = row_a.shape[0]
    bins = feats.shape[0]
    row_start = pos[0] * rows
    col_start = pos[1] * width
    odd_row = pos[0] % 2 == 1
    odd_col = pos[1] % 2 == 1
    all_feats = feats[...]
    own_feats[...] = pick_bins(all_feats, row_start - rim, 1)[:channels]
    col_feats = [
        pick_bins(all_feats, col_start + h * half - rim, 1)[:channels] for h in range(2)
    ]
    lane_in = [inside(col_start + h * half - rim, 1, bins) for h in range(2)]
    lane = lanes((channels, width))
    total = rows + 2 * rim
    for e in range(total):
        if e < rim:
            x = jnp.where(odd_row, row_a[e], row_b[e])
        elif e < rim + rows:
            x = center[e - rim]
        else:
            x = jnp.where(odd_row, row_b[e - rim - rows], row_a[e - rim - rows])
        x = x.astype(f32)
        group, k = divmod(e, 16)
        pa = col_a[group].astype(f32)
        pb = col_b[group].astype(f32)
        left = jnp.where(odd_col, pa, pb)
        right = jnp.where(odd_col, pb, pa)
        halves = (
            jnp.where(lane < rim, roll(left, -(8 * k + 8 - rim)), roll(x, rim)),
            jnp.where(lane < half + rim, roll(x, rim - half), roll(right, half + rim - 8 * k)),
        )
        ok = scalar_inside(row_start - rim + e, bins)
        own = own_feats[:, e : e + 1]
        for h in range(2):
            value = (halves[h] + (col_feats[h] + own)) * (lane_in[h] * ok)
            store_taps(s1, e, h * 128, value, 2)
    w1 = weights[0]
    b1 = bias[0]
    mask1 = jnp.concatenate(
        [inside(col_start + h * half - rim + 2, 1, bins) for h in range(2)], axis=1
    )

    products(w1, s1, parts, total)

    def first(e, carry):
        value = jnp.maximum(combine(parts, e, 2) + b1, 0.0)
        ok = scalar_inside(row_start - rim + 2 + e, bins)
        value = value * (mask1 * ok)
        for h in range(2):
            store_taps(s2, e, h * 128, value[:, h * 128 : h * 128 + 128], 4)
        return carry

    lax.fori_loop(0, total - 4, first, 0, unroll=4)
    w2 = weights[1]
    b2 = bias[1]

    products(w2, s2, parts, total - 4)
    low = lane < half
    messages = ((m00, m01), (m10, m11))
    upper = 2 * row_start < bins
    for u in range(2):

        def produce(p, carry, u=u):
            q = rows // 2 * u + 2 * p
            even = jnp.maximum(combine(parts, q, 4) + b2, 0.0)
            odd = jnp.maximum(combine(parts, q + 1, 4) + b2, 0.0)
            for t, value in ((0, even), (1, odd)):
                coarse[q + t] = jnp.where(
                    low, value[:, :128], roll(value[:, 128:], half)
                ).astype(bf16)
            sides = [
                jnp.where(
                    low,
                    even[:, v * 128 : v * 128 + 128],
                    roll(odd[:, v * 128 : v * 128 + 128], half),
                ).astype(bf16)
                for v in range(2)
            ]

            @pl.when(upper)
            def _():
                for v in range(2):
                    messages[u][v][p] = sides[v]

            @pl.when(jnp.logical_not(upper))
            def _():
                for v in range(2):
                    messages[1 - u][1 - v][p] = sides[v]

            return carry

        lax.fori_loop(0, rows // 4, produce, 0, unroll=4)


def strip_pack_window(pos, center, row_a, row_b, out_a, out_b):
    rim = row_a.shape[0]
    pairs = center.shape[0]
    odd_row = pos[0] % 2 == 1
    odd_col = pos[1] % 2 == 1
    slot = lanes(row_a.shape[1:]) % 64 // 16
    for group in range(out_a.shape[0]):
        packed_a = jnp.zeros(row_a.shape[1:], f32)
        packed_b = packed_a
        for m in range(4):
            g = group * 4 + m
            if g < rim:
                x = jnp.where(odd_row, row_a[g], row_b[g])
            elif g < rim + pairs:
                x = center[g - rim]
            else:
                x = jnp.where(odd_row, row_b[g - rim - pairs], row_a[g - rim - pairs])
            x = x.astype(f32)
            turned = roll(x, 80)
            here = slot == m
            packed_a = jnp.where(here, roll(jnp.where(odd_col, x, turned), 16 * m), packed_a)
            packed_b = jnp.where(here, roll(jnp.where(odd_col, turned, x), 16 * m), packed_b)
        out_a[group] = packed_a.astype(bf16)
        out_b[group] = packed_b.astype(bf16)


def fine_kernel(pos, row_weights, col_weights, bias, feats, row_terms, col_terms, parts):
    channels = bias.shape[0]
    bins = feats.shape[0]
    row_start = pos[0] * pos[2]
    col_start = pos[1] * pos[3]
    all_feats = feats[...]

    def stacked(start, step, shift):
        picked = pick_bins(all_feats, start, step)[channels:]
        taps = [roll(picked, -shift * tap) for tap in range(3)]
        return jnp.concatenate(taps, 0).astype(bf16)

    parts[...] = dot(row_weights[...], stacked(row_start - 24, 1, 8))
    at = col_start - 16 + 2 * lanes((1, 128))
    left_in = ((at >= 8) & (at < bins + 8)).astype(f32)
    right_in = ((at >= -8) & (at < bins - 8)).astype(f32)
    b = bias[...]
    for n in range(row_terms.shape[0]):
        row_terms[n] = (
            parts[channels : 2 * channels, n : n + 1]
            + b
            + parts[:channels, n : n + 1] * left_in
            + parts[2 * channels :, n : n + 1] * right_in
        )
    for v in range(2):
        terms = dot(col_weights[...], stacked(col_start - 24 + v, 2, 4))
        for a in range(3):
            col_terms[v, a] = terms[a * channels : (a + 1) * channels]


def refine_kernel(
    pos, weights, weights2, bias2, center, row_a, row_b, col_a, col_b, row_terms, col_terms,
    refined, sw, sh, products_w, products_h,
):
    pairs, channels, _ = center.shape
    rim = row_a.shape[0]
    rows, cols, bins = pos[2], pos[3], pos[4]
    row_start = pos[0] * rows
    col_start = pos[1] * cols
    odd_row = pos[0] % 2 == 1
    odd_col = pos[1] % 2 == 1
    lane = lanes((channels, 128))
    total = pairs + 2 * rim
    for g in range(total):
        if g < rim:
            x = jnp.where(odd_row, row_a[g], row_b[g])
        elif g < rim + pairs:
            x = center[g - rim]
        else:
            x = jnp.where(odd_row, row_b[g - rim - pairs], row_a[g - rim - pairs])
        x = x.astype(f32)
        group, m = divmod(g, 4)
        pa = col_a[group].astype(f32)
        pb = col_b[group].astype(f32)
        left = jnp.where(odd_col, pa, pb)
        right = jnp.where(odd_col, pb, pa)
        for t in range(2):
            base = 64 * t + 16 * m
            value = jnp.where(
                lane < 12,
                roll(left, -(base + 4)),
                jnp.where(lane < 76, roll(x, 12 - 64 * t), roll(right, 76 - base)),
            )
            store_taps(sw, g, t * 128, value, 4)
    w1 = weights[...]
    col_in = inside(col_start - 16, 2, bins)
    low = lane < 64

    products(w1, sw, products_w, total)

    def first(n, carry):
        both = combine(products_w, n, 2)
        for t in range(2):
            k = 2 * n + t
            base = both[:, t * 128 : t * 128 + 128]
            at = row_start - 16 + 2 * k
            above = scalar_inside(at - 8, bins)
            below = scalar_inside(at + 8, bins)
            mask = col_in * scalar_inside(at, bins)
            sums = [
                base + (col_terms[v, 1] + col_terms[v, 0] * above + col_terms[v, 2] * below)
                for v in range(2)
            ]
            for u in range(2):
                own = row_terms[2 * k + u]
                h = [jnp.maximum(s + own, 0.0) * mask for s in sums]
                for tap in range(3):
                    sh[k, tap * channels : (tap + 1) * channels, u * 128 : u * 128 + 128] = (
                        jnp.where(low, roll(h[0], -8 * tap), roll(h[1], 64 - 8 * tap)).astype(bf16)
                    )
        return carry

    inner = total - 4
    lax.fori_loop(0, inner, first, 0, unroll=2)
    w2 = weights2[...]
    b2 = bias2[...]

    products(w2, sh, products_h, sh.shape[0])
    source = lax.broadcasted_iota(jnp.int32, (128, 128), 0)
    spread = 2 * (source % 64) + source // 64 == lanes((128, 128))
    spread = spread.astype(f32).astype(bf16)

    def produce(p, carry):
        value = jnp.maximum(combine(products_h, p, 8) + b2, 0.0).astype(bf16)
        both = jnp.concatenate([value[:, :128], value[:, 128:]], axis=0)
        both = dot(both, spread).astype(bf16)
        refined[2 * p] = both[:channels]
        refined[2 * p + 1] = both[channels:]
        return carry

    lax.fori_loop(0, 2 * pairs, produce, 0, unroll=4)


def per_device(
    coarse_feats, fine_feats, pair_prior, zoom_start, coarse_weights, coarse_bias,
    refine_first, refine_second, refine_bias,
):
    channels, rows, cols = pair_prior.shape
    row_count = lax.axis_size("row")
    col_count = lax.axis_size("col")
    bins = rows * row_count
    row_place = lax.axis_index("row")
    col_place = lax.axis_index("col")
    pos = jnp.stack(
        [row_place, col_place, jnp.int32(rows), jnp.int32(cols), jnp.int32(bins)]
    ).astype(jnp.int32)
    odd_row = row_place % 2 == 1
    devices = row_count * col_count

    own = jnp.concatenate([coarse_feats, fine_feats], axis=0).T
    spread = jnp.broadcast_to(own[None], (devices,) + own.shape)
    feats = lax.all_to_all(spread, ("row", "col"), split_axis=0, concat_axis=0, tiled=True)
    feats = feats.reshape(bins, 2 * channels)

    def row_swap(block, rim):
        top, bottom = block[:rim], block[block.shape[0] - rim :]
        first, second = swap_pairs(row_count)
        return (
            lax.ppermute(jnp.where(odd_row, top, bottom), "row", first),
            lax.ppermute(jnp.where(odd_row, bottom, top), "row", second),
        )

    def col_swap(a, b):
        first, second = swap_pairs(col_count)
        return lax.ppermute(a, "col", first), lax.ppermute(b, "col", second)

    def struct(shape, dtype=bf16):
        return jax.ShapeDtypeStruct(shape, dtype)

    rim = 6
    center = jnp.transpose(pair_prior, (1, 0, 2))
    row_a, row_b = row_swap(center, rim)
    total = rows + 2 * rim
    pack = struct((pl.cdiv(total, 16), channels, 128))
    col_a, col_b = col_swap(
        *call(strip_pack_tile, (pack, pack), [], (1 << 20, 2 << 20), "tile_strips")(
            pos, center, row_a, row_b
        )
    )
    stacked = 3 * channels

    message = struct((rows // 4, channels, 128))
    coarse, *messages = call(
        tile_kernel,
        (struct((rows, channels, cols)),) + (message,) * 4,
        [
            pltpu.VMEM((total, stacked, 256), bf16),
            pltpu.VMEM((total, stacked, 256), bf16),
            pltpu.VMEM((total, stacked, 256), f32),
            pltpu.VMEM((channels, 128), f32),
        ],
        (3 << 30, 4 << 20),
        "tile",
    )(
        pos,
        coarse_weights.reshape(2, stacked, stacked),
        coarse_bias[:, :, None],
        feats, center, row_a, row_b, col_a, col_b,
    )

    half_rows, half_cols = row_count // 2, col_count // 2
    received = []
    for u in range(2):
        for v in range(2):
            pairs = []
            for a in range(half_rows):
                for b in range(half_cols):
                    pairs.append((a * col_count + b, (2 * a + u) * col_count + 2 * b + v))
                    pairs.append(
                        (
                            (half_rows + a) * col_count + half_cols + b,
                            (2 * a + 1 - u) * col_count + 2 * b + 1 - v,
                        )
                    )
            received.append(lax.ppermute(messages[2 * u + v], ("row", "col"), pairs))
    quarter = 2 * (row_place % 2) + col_place % 2
    quarter = jnp.where(zoom_start[0] > 0, 3 - quarter, quarter)
    window = jnp.where(
        quarter < 2,
        jnp.where(quarter == 0, received[0], received[1]),
        jnp.where(quarter == 2, received[2], received[3]),
    )

    parts = refine_first.reshape(3, channels, 3, 2 * channels)
    window_weights = parts[..., :channels].reshape(stacked, stacked)
    fine_parts = parts[..., channels:]
    row_terms, col_terms = call(
        fine_kernel,
        (struct((rows + 32, channels, 128), f32), struct((2, 3, channels, 128), f32)),
        [pltpu.VMEM((stacked, 128), f32)],
        (1 << 28, 4 << 20),
        "fine",
    )(
        pos,
        fine_parts.transpose(2, 1, 0, 3).reshape(stacked, stacked),
        fine_parts.reshape(stacked, stacked),
        refine_bias[0][:, None],
        feats,
    )

    window_rim = 6
    row_a, row_b = row_swap(window, window_rim)
    pairs = rows // 4 + 2 * window_rim
    pack = struct((pairs // 4, channels, 128))
    col_a, col_b = col_swap(
        *call(strip_pack_window, (pack, pack), [], (1 << 20, 1 << 20), "window_strips")(
            pos, window, row_a, row_b
        )
    )
    fine_rows = rows // 2 + 16
    refined = call(
        refine_kernel,
        struct((rows, channels, cols)),
        [
            pltpu.VMEM((pairs, stacked, 256), bf16),
            pltpu.VMEM((fine_rows, stacked, 256), bf16),
            pltpu.VMEM((pairs, stacked, 256), f32),
            pltpu.VMEM((fine_rows, stacked, 256), f32),
        ],
        (3 << 30, 6 << 20),
        "refine",
    )(
        pos,
        window_weights,
        refine_second.reshape(stacked, stacked),
        refine_bias[1][:, None],
        window, row_a, row_b, col_a, col_b, row_terms, col_terms,
    )
    return jnp.transpose(coarse, (1, 0, 2)), jnp.transpose(refined, (1, 0, 2))


def solution(mesh):
    return jax.shard_map(
        per_device,
        mesh=mesh,
        in_specs=(
            P(None, ("row", "col")),
            P(None, ("row", "col")),
            P(None, "row", "col"),
            P(),
            P(),
            P(),
            P(),
            P(),
            P(),
        ),
        out_specs=(P(None, "row", "col"), P(None, "row", "col")),
        check_vma=False,
    )
```

```python
import functools

import jax
import jax.numpy as jnp
from jax import lax
from jax.experimental import pallas as pl
from jax.experimental.pallas import tpu as pltpu
from jax.sharding import PartitionSpec as P

f32 = jnp.float32
bf16 = jnp.bfloat16
VMEM = pl.BlockSpec(memory_space=pltpu.VMEM)
SMEM = pl.BlockSpec(memory_space=pltpu.SMEM)


def call(body, outs, scratch, cost, name):
    flops, moved = cost
    def run(*args):
        return pl.pallas_call(
            body,
            out_shape=outs,
            in_specs=[SMEM] + [VMEM] * (len(args) - 1),
            out_specs=jax.tree.map(lambda _: VMEM, outs),
            scratch_shapes=scratch,
            compiler_params=pltpu.CompilerParams(vmem_limit_bytes=56 << 20),
            cost_estimate=pl.CostEstimate(flops=flops, bytes_accessed=moved, transcendentals=0),
            name=name,
        )(*args)

    return run


def roll(x, shift):
    shift = shift % x.shape[-1]
    return x if shift == 0 else pltpu.roll(x, shift, x.ndim - 1)


def lanes(shape):
    return lax.broadcasted_iota(jnp.int32, shape, len(shape) - 1)


def swap_pairs(count):
    first = [(i, i ^ 1) for i in range(count)]
    second = [(i, i + 1) for i in range(1, count - 1, 2)]
    return first, second + [(b, a) for a, b in second]


def dot(a, b):
    return jnp.dot(a, b, preferred_element_type=f32)


def one_hot(hit):
    return hit.astype(f32).astype(bf16)


def pick_at(feats, index):
    shape = (feats.shape[1], 128)
    return dot(feats, one_hot(lax.broadcasted_iota(jnp.int32, shape, 0) == index))


def pick_bins(feats, start, step):
    return pick_at(feats, start + step * lanes((1, 128)))


def source_and_target(sources, targets):
    shape = (sources, targets)
    return lax.broadcasted_iota(jnp.int32, shape, 0), lanes(shape)


def within(at, bins):
    return ((at >= 0) & (at < bins)).astype(f32)


def inside(start, step, bins, shape=(1, 128)):
    at = start + step * lanes(shape)
    return ((at >= 0) & (at < bins)).astype(f32)


def scalar_inside(at, bins):
    return ((at >= 0) & (at < bins)).astype(f32)


def ext_row(e, odd_row, center, row_a, row_b):
    rim, count = row_a.shape[0], center.shape[0]
    if e < rim:
        return jnp.where(odd_row, row_a[e], row_b[e])
    if e < rim + count:
        return center[e - rim]
    return jnp.where(odd_row, row_b[e - rim - count], row_a[e - rim - count])


def pair_kernel(pos, feats, center, row_a, row_b, pair, out_a, out_b, own_feats):
    rim, channels, width = row_a.shape
    rows = center.shape[0]
    bins = feats.shape[1]
    row_start = pos[0] * rows
    odd_row = pos[0] % 2 == 1
    odd_col = pos[1] % 2 == 1
    total = rows + 2 * rim
    all_feats = feats[:channels]
    own_feats[...] = pick_bins(all_feats, row_start - rim, 1)
    col_feats = pick_bins(all_feats, pos[1] * width, 1)
    source, target = source_and_target(width, 2 * width)
    last = (target >= width) == odd_col
    copies = one_hot(source == target % 8 + jnp.where(last, width - 8, 0))
    slot = lanes((channels, width)) // 8
    for group in range(out_a.shape[0]):
        size = min(16, total - group * 16)
        blocks = []
        for k in range(size):
            e = group * 16 + k
            x = ext_row(e, odd_row, center, row_a, row_b).astype(f32)
            value = x + (col_feats + own_feats[:, e : e + 1])
            if e < rim or e >= rim + rows:
                value = value * scalar_inside(row_start - rim + e, bins)
            blocks.append(value.astype(bf16))
            pair[e] = blocks[-1]
        spread = dot(jnp.concatenate(blocks, axis=0), copies)
        for out, first in ((out_a, 0), (out_b, width)):
            parts = [
                jnp.where(
                    slot == k,
                    spread[k * channels : (k + 1) * channels, first : first + width],
                    0.0,
                )
                for k in range(size)
            ]
            while len(parts) > 1:
                parts = [sum(parts[i : i + 2]) for i in range(0, len(parts), 2)]
            out[group] = parts[0].astype(bf16)


def products(weights, taps, out, count):
    def one(row, carry):
        out[row] = dot(weights, taps[row])
        return carry

    lax.fori_loop(0, count, one, 0, unroll=4)


def combine(parts, row, spacing):
    size = parts.shape[1] // 3
    return (
        parts[row, :size]
        + parts[row + spacing, size : 2 * size]
        + parts[row + 2 * spacing, 2 * size :]
    )


def tile_kernel(
    turn, pos, weights, bias, pair, col_a, col_b, m0, m1, s1, s2, parts,
):
    total, channels, width = pair.shape
    half = width // 2
    rows, bins = pos[2], pos[4]
    rim = 6
    row_start = pos[0] * rows
    col_start = pos[1] * width
    odd_col = pos[1] % 2 == 1
    upper = 2 * row_start < bins
    first_col = half * jnp.where(upper, turn, 1 - turn) - rim
    lane = lanes((channels, width))
    slot = lane // 8
    source, target = source_and_target(2 * width, 3 * width)
    col = target % width + 2 * (target // width) + first_col
    inner = (source == col) & (source < width)
    strip = source - width
    near = strip < half
    on_left = (strip % 8 == col + 8) & (col < 0)
    on_right = (strip % 8 == col - width) & (col >= width)
    strip_ok = strip >= 0
    move = [
        one_hot(inner | (strip_ok & ((near & on_left) | (~near & on_right)))),
        one_hot(inner | (strip_ok & ((~near & on_left) | (near & on_right)))),
    ]
    for group in range(col_a.shape[0]):
        pa = col_a[group].astype(f32)
        pb = col_b[group].astype(f32)
        left = jnp.where(odd_col, pa, pb)
        right = roll(jnp.where(odd_col, pb, pa), half)
        for quad in range(4):
            blocks = []
            for k in range(4 * quad, 4 * quad + 4):
                e = 16 * group + k
                if e >= total:
                    break
                edge = jnp.where(slot == k, left, jnp.where(slot == (k + 8) % 16, right, 0.0))
                blocks.append(jnp.concatenate([pair[e], edge.astype(bf16)], axis=1))
            if not blocks:
                break
            moved = dot(jnp.concatenate(blocks, axis=0), move[quad // 2]).astype(bf16)
            for i in range(len(blocks)):
                e = 16 * group + 4 * quad + i
                for tap in range(3):
                    s1[
                        e // 2,
                        tap * channels : (tap + 1) * channels,
                        e % 2 * width : (e % 2 + 1) * width,
                    ] = moved[i * channels : (i + 1) * channels, tap * width : (tap + 1) * width]
    b1 = bias[0]
    mask1 = inside(col_start + first_col + 2, 1, bins)
    products(weights[0], s1, parts, total // 2)
    source, target = source_and_target(width, 2 * width)
    shift = one_hot(source == target % width + 4 * (target // width + 1))

    def first(c, carry):
        blocks = []
        for i in range(2):
            g = 2 * c + i
            value = jnp.maximum(combine(parts, g, 1) + b1, 0.0)
            for t in range(2):
                ok = scalar_inside(row_start - rim + 2 + 2 * g + t, bins)
                block = (value[:, t * width : (t + 1) * width] * (mask1 * ok)).astype(bf16)
                s2[g, :channels, t * width : (t + 1) * width] = block
                blocks.append(block)
        moved = dot(jnp.concatenate(blocks, axis=0), shift).astype(bf16)
        for j in range(4):
            for tap in (1, 2):
                s2[
                    2 * c + j // 2,
                    tap * channels : (tap + 1) * channels,
                    j % 2 * width : (j % 2 + 1) * width,
                ] = moved[j * channels : (j + 1) * channels, (tap - 1) * width : tap * width]
        return carry

    lax.fori_loop(0, (total - 4) // 4, first, 0, unroll=6)
    b2 = bias[1]
    products(weights[1], s2, parts, total // 2 - 2)
    low = lane < half
    quarter = m0.shape[0]
    for message, begin in (
        (m0, jnp.where(upper, 0, quarter)),
        (m1, jnp.where(upper, quarter, 0)),
    ):

        def produce(p, carry, message=message, begin=begin):
            value = jnp.maximum(combine(parts, begin + p, 2) + b2, 0.0)
            message[p] = jnp.where(low, value[:, :width], roll(value[:, width:], half)).astype(bf16)
            return carry

        lax.fori_loop(0, quarter, produce, 0, unroll=8)


def assemble_kernel(pos, m00, m01, m10, m11, coarse):
    quarter, channels, width = m00.shape
    half = width // 2
    upper = 2 * pos[0] < pos[4] // pos[2]
    low = lanes((channels, width)) < half
    for u in range(2):

        def pair(p, carry, u=u):
            sides = [
                jnp.where(upper, (m00, m01, m10, m11)[2 * u + v][p], (m11, m10, m01, m00)[2 * u + v][p])
                for v in range(2)
            ]
            left, right = [side.astype(f32) for side in sides]
            at = 2 * (quarter * u + p)
            coarse[at] = jnp.where(low, left, roll(right, half)).astype(bf16)
            coarse[at + 1] = jnp.where(low, roll(left, half), right).astype(bf16)
            return carry

        lax.fori_loop(0, quarter, pair, 0, unroll=4)


def strip_pack_window(pos, center, row_a, row_b, out_a, out_b):
    rim, channels, width = row_a.shape
    half = width // 2
    odd_row = pos[0] % 2 == 1
    odd_col = pos[1] % 2 == 1
    source, target = source_and_target(width, 2 * width)
    last = (target >= width) == odd_col
    spot = target % width
    copies = one_hot(
        source == spot // half * half + spot % 16 + jnp.where(last, half - 16, 0)
    )
    slot = lanes((channels, width)) % half // 16
    for group in range(out_a.shape[0]):
        block = jnp.concatenate(
            [ext_row(group * 4 + m, odd_row, center, row_a, row_b) for m in range(4)], axis=0
        )
        spread = dot(block, copies)
        for out, first in ((out_a, 0), (out_b, width)):
            parts = [spread[m * channels : (m + 1) * channels, first : first + width] for m in range(4)]
            out[group] = jnp.where(
                slot < 2,
                jnp.where(slot == 0, parts[0], parts[1]),
                jnp.where(slot == 2, parts[2], parts[3]),
            ).astype(bf16)


def fine_kernel(pos, row_weights, col_weights, bias, feats, row_terms, col_terms, terms):
    channels = bias.shape[0]
    bins = feats.shape[1]
    row_start = pos[0] * pos[2]
    col_start = pos[1] * pos[3]
    all_feats = feats[channels:]

    def stacked(start, step, shift):
        picked = pick_bins(all_feats, start, step)
        return jnp.concatenate([roll(picked, -shift * tap) for tap in range(3)], 0).astype(bf16)

    parts = dot(row_weights[...], stacked(row_start - 24, 1, 8))
    taps = [parts[e * channels : (e + 1) * channels] for e in range(3)]
    at_left = pos[1] == 0
    at = col_start - 16 + 2 * lanes((channels, 128))
    inside_taps = ((at_left) | (at < bins - 8)) & (jnp.logical_not(at_left) | (at >= 8))
    terms[0] = taps[0] + taps[1] + taps[2] + bias[...]
    terms[1] = taps[1] + jnp.where(at_left, taps[2], taps[0]) + bias[...]
    for n in range(row_terms.shape[0]):
        row_terms[n] = jnp.where(inside_taps, terms[0, :, n : n + 1], terms[1, :, n : n + 1])
    for v in range(2):
        across = dot(col_weights[...], stacked(col_start - 24 + v, 2, 4))
        for a in range(3):
            col_terms[v, a] = across[a * channels : (a + 1) * channels]


def refine_kernel(
    pos, weights, weights2, bias2, center, row_a, row_b, col_a, col_b, row_terms, col_terms,
    refined, sw, sh, products_w, products_h,
):
    pairs, channels, _ = center.shape
    rim = row_a.shape[0]
    rows, cols, bins = pos[2], pos[3], pos[4]
    row_start = pos[0] * rows
    col_start = pos[1] * cols
    odd_row = pos[0] % 2 == 1
    odd_col = pos[1] % 2 == 1
    total = pairs + 2 * rim
    slot = lanes((channels, 128)) % 64 // 16
    source, target = source_and_target(384, 768)
    tap, t = target // 128 % 3, target // 384
    col = target % 128 + 4 * tap - 12
    spot = source % 128
    same = spot // 64 == t
    place = source // 128
    move = one_hot(
        same
        & (
            ((place == 0) & (spot % 64 == col))
            | ((place == 1) & (spot % 16 == col + 16) & (col < 0))
            | ((place == 2) & (spot % 16 == col - 64) & (col >= 64))
        )
    )
    for group in range(col_a.shape[0]):
        pa, pb = col_a[group].astype(f32), col_b[group].astype(f32)
        left = jnp.where(odd_col, pa, pb)
        right = jnp.where(odd_col, pb, pa)
        blocks = []
        for m in range(4):
            x = ext_row(4 * group + m, odd_row, center, row_a, row_b)
            here = slot == m
            blocks.append(
                jnp.concatenate(
                    [x]
                    + [jnp.where(here, side, 0.0).astype(bf16) for side in (left, right)],
                    axis=1,
                )
            )
        moved = dot(jnp.concatenate(blocks, axis=0), move).astype(bf16)
        for m in range(4):
            for j in range(6):
                sw[
                    4 * group + m,
                    j % 3 * channels : (j % 3 + 1) * channels,
                    j // 3 * 128 : (j // 3 + 1) * 128,
                ] = moved[m * channels : (m + 1) * channels, j * 128 : (j + 1) * 128]
    w1 = weights[...]
    col_in = inside(col_start - 16, 2, bins)
    source, target = source_and_target(256, 384)
    spot = target % 128
    spread = one_hot(source == spot // 64 * 128 + spot % 64 + 8 * (target // 128))
    products(w1, sw, products_w, total)

    def first(n, carry):
        both = combine(products_w, n, 2)
        blocks = []
        for t in range(2):
            k = 2 * n + t
            base = both[:, t * 128 : t * 128 + 128]
            at = row_start - 16 + 2 * k
            above = scalar_inside(at - 8, bins)
            below = scalar_inside(at + 8, bins)
            mask = col_in * scalar_inside(at, bins)
            sums = [
                base + (col_terms[v, 1] + col_terms[v, 0] * above + col_terms[v, 2] * below)
                for v in range(2)
            ]
            for u in range(2):
                own = row_terms[2 * k + u]
                h = [(jnp.maximum(s + own, 0.0) * mask).astype(bf16) for s in sums]
                blocks.append(jnp.concatenate(h, axis=1))
        moved = dot(jnp.concatenate(blocks, axis=0), spread).astype(bf16)
        for j in range(4):
            for tap in range(3):
                sh[
                    2 * n + j // 2,
                    tap * channels : (tap + 1) * channels,
                    j % 2 * 128 : (j % 2 + 1) * 128,
                ] = moved[j * channels : (j + 1) * channels, tap * 128 : (tap + 1) * 128]
        return carry

    inner = total - 4
    lax.fori_loop(0, inner, first, 0, unroll=6)
    w2 = weights2[...]
    b2 = bias2[...]

    products(w2, sh, products_h, sh.shape[0])
    source, target = source_and_target(128, 128)
    weave = one_hot(2 * (source % 64) + source // 64 == target)

    def produce(p, carry):
        value = jnp.maximum(combine(products_h, p, 8) + b2, 0.0).astype(bf16)
        both = jnp.concatenate([value[:, :128], value[:, 128:]], axis=0)
        both = dot(both, weave).astype(bf16)
        refined[2 * p] = both[:channels]
        refined[2 * p + 1] = both[channels:]
        return carry

    lax.fori_loop(0, 2 * pairs, produce, 0, unroll=8)


def per_device(
    coarse_feats, fine_feats, pair_prior, zoom_start, coarse_weights, coarse_bias,
    refine_first, refine_second, refine_bias,
):
    channels, rows, cols = pair_prior.shape
    row_count = lax.axis_size("row")
    col_count = lax.axis_size("col")
    bins = rows * row_count
    row_place = lax.axis_index("row")
    col_place = lax.axis_index("col")
    pos = jnp.stack(
        [row_place, col_place, jnp.int32(rows), jnp.int32(cols), jnp.int32(bins)]
    ).astype(jnp.int32)
    odd_row = row_place % 2 == 1
    devices = row_count * col_count

    own = jnp.concatenate([coarse_feats, fine_feats], axis=0).T
    spread = jnp.broadcast_to(own[None], (devices,) + own.shape)
    feats = lax.all_to_all(spread, ("row", "col"), split_axis=0, concat_axis=0, tiled=True)
    feats = feats.reshape(bins, 2 * channels).T

    def row_swap(block, rim):
        top, bottom = block[:rim], block[block.shape[0] - rim :]
        first, second = swap_pairs(row_count)
        return (
            lax.ppermute(jnp.where(odd_row, top, bottom), "row", first),
            lax.ppermute(jnp.where(odd_row, bottom, top), "row", second),
        )

    def col_swap(a, b):
        first, second = swap_pairs(col_count)
        return lax.ppermute(a, "col", first), lax.ppermute(b, "col", second)

    def struct(shape, dtype=bf16):
        return jax.ShapeDtypeStruct(shape, dtype)

    rim = 6
    center = jnp.transpose(pair_prior, (1, 0, 2))
    row_a, row_b = row_swap(center, rim)
    total = rows + 2 * rim
    pack = struct((pl.cdiv(total, 16), channels, 128))
    pair, *packs = call(
        pair_kernel,
        (struct((total, channels, cols)), pack, pack),
        [pltpu.VMEM((channels, 128), f32)],
        (1 << 28, 4 << 20),
        "pair",
    )(pos, feats, center, row_a, row_b)
    col_a, col_b = col_swap(*packs)
    stacked = 3 * channels

    message = struct((rows // 4, channels, 128))
    tile_weights = coarse_weights.reshape(2, stacked, stacked)
    tile_bias = coarse_bias[:, :, None]
    halves = [
        call(
            functools.partial(tile_kernel, turn),
            (message,) * 2,
            [
                pltpu.VMEM((total // 2, stacked, 256), bf16),
                pltpu.VMEM((total // 2, stacked, 256), bf16),
                pltpu.VMEM((total // 2, stacked, 256), f32),
            ],
            (3 << 30, 3 << 20),
            f"tile{turn}",
        )(
            pos, tile_weights, tile_bias, pair, col_a, col_b
        )
        for turn in range(2)
    ]
    messages = [halves[v][u] for u in range(2) for v in range(2)]
    coarse = call(
        assemble_kernel, struct((rows, channels, cols)), [], (1 << 20, 2 << 20), "assemble"
    )(pos, *messages)

    half_rows, half_cols = row_count // 2, col_count // 2
    received = [None] * 4
    for v in range(2):
        for u in range(2):
            pairs = []
            for a in range(half_rows):
                for b in range(half_cols):
                    pairs.append((a * col_count + b, (2 * a + u) * col_count + 2 * b + v))
                    pairs.append(
                        (
                            (half_rows + a) * col_count + half_cols + b,
                            (2 * a + 1 - u) * col_count + 2 * b + 1 - v,
                        )
                    )
            received[2 * u + v] = lax.ppermute(messages[2 * u + v], ("row", "col"), pairs)
    quarter = 2 * (row_place % 2) + col_place % 2
    quarter = jnp.where(zoom_start[0] > 0, 3 - quarter, quarter)
    window = jnp.where(
        quarter < 2,
        jnp.where(quarter == 0, received[0], received[1]),
        jnp.where(quarter == 2, received[2], received[3]),
    )

    parts = refine_first.reshape(3, channels, 3, 2 * channels)
    window_weights = parts[..., :channels].reshape(stacked, stacked)
    fine_parts = parts[..., channels:]
    row_terms, col_terms = call(
        fine_kernel,
        (struct((rows + 32, channels, 128), f32), struct((2, 3, channels, 128), f32)),
        [pltpu.VMEM((2, channels, 128), f32)],
        (1 << 28, 4 << 20),
        "fine",
    )(
        pos,
        fine_parts.transpose(2, 1, 0, 3).reshape(stacked, stacked),
        fine_parts.reshape(stacked, stacked),
        refine_bias[0][:, None],
        feats,
    )

    coarse = jnp.transpose(coarse, (1, 0, 2))
    second_weights = refine_second.reshape(stacked, stacked)
    second_bias = refine_bias[1][:, None]
    window, coarse, row_terms, col_terms, window_weights, second_weights, second_bias = (
        lax.optimization_barrier(
            (window, coarse, row_terms, col_terms, window_weights, second_weights, second_bias)
        )
    )
    window_rim = 6
    row_a, row_b = row_swap(window, window_rim)
    pairs = rows // 4 + 2 * window_rim
    pack = struct((pairs // 4, channels, 128))
    col_a, col_b = col_swap(
        *call(strip_pack_window, (pack, pack), [], (1 << 20, 1 << 20), "window_strips")(
            pos, window, row_a, row_b
        )
    )
    fine_rows = rows // 2 + 16
    refined = call(
        refine_kernel,
        struct((rows, channels, cols)),
        [
            pltpu.VMEM((pairs, stacked, 256), bf16),
            pltpu.VMEM((fine_rows, stacked, 256), bf16),
            pltpu.VMEM((pairs, stacked, 256), f32),
            pltpu.VMEM((fine_rows, stacked, 256), f32),
        ],
        (3 << 30, 6 << 20),
        "refine",
    )(
        pos,
        window_weights,
        second_weights,
        second_bias,
        window, row_a, row_b, col_a, col_b, row_terms, col_terms,
    )
    return coarse, jnp.transpose(refined, (1, 0, 2))


def solution(mesh):
    return jax.shard_map(
        per_device,
        mesh=mesh,
        in_specs=(
            P(None, ("row", "col")),
            P(None, ("row", "col")),
            P(None, "row", "col"),
            P(),
            P(),
            P(),
            P(),
            P(),
            P(),
        ),
        out_specs=(P(None, "row", "col"), P(None, "row", "col")),
        check_vma=False,
    )
```

```python
import functools

import jax
import jax.numpy as jnp
from jax import lax
from jax.experimental import pallas as pl
from jax.experimental.pallas import tpu as pltpu
from jax.sharding import PartitionSpec as P

f32 = jnp.float32
bf16 = jnp.bfloat16
VMEM = pl.BlockSpec(memory_space=pltpu.VMEM)
SMEM = pl.BlockSpec(memory_space=pltpu.SMEM)


def call(body, outs, scratch, cost, name):
    flops, moved = cost
    def run(*args):
        return pl.pallas_call(
            body,
            out_shape=outs,
            in_specs=[SMEM] + [VMEM] * (len(args) - 1),
            out_specs=jax.tree.map(lambda _: VMEM, outs),
            scratch_shapes=scratch,
            compiler_params=pltpu.CompilerParams(vmem_limit_bytes=44 << 20),
            cost_estimate=pl.CostEstimate(flops=flops, bytes_accessed=moved, transcendentals=0),
            name=name,
        )(*args)

    return run


def roll(x, shift):
    shift = shift % x.shape[-1]
    return x if shift == 0 else pltpu.roll(x, shift, x.ndim - 1)


def lanes(shape):
    return lax.broadcasted_iota(jnp.int32, shape, len(shape) - 1)


def swap_pairs(count):
    first = [(i, i ^ 1) for i in range(count)]
    second = [(i, i + 1) for i in range(1, count - 1, 2)]
    return first, second + [(b, a) for a, b in second]


def dot(a, b):
    return jnp.dot(a, b, preferred_element_type=f32)


def one_hot(hit):
    return hit.astype(f32).astype(bf16)


def pick_at(feats, index):
    shape = (feats.shape[1], 128)
    return dot(feats, one_hot(lax.broadcasted_iota(jnp.int32, shape, 0) == index))


def pick_bins(feats, start, step):
    return pick_at(feats, start + step * lanes((1, 128)))


def source_and_target(sources, targets):
    shape = (sources, targets)
    return lax.broadcasted_iota(jnp.int32, shape, 0), lanes(shape)


def within(at, bins):
    return ((at >= 0) & (at < bins)).astype(f32)


def inside(start, step, bins, shape=(1, 128)):
    at = start + step * lanes(shape)
    return ((at >= 0) & (at < bins)).astype(f32)


def scalar_inside(at, bins):
    return ((at >= 0) & (at < bins)).astype(f32)


def ext_row(e, odd_row, center, row_a, row_b):
    rim, count = row_a.shape[0], center.shape[0]
    if e < rim:
        return jnp.where(odd_row, row_a[e], row_b[e])
    if e < rim + count:
        return center[e - rim]
    return jnp.where(odd_row, row_b[e - rim - count], row_a[e - rim - count])


def pair_kernel(pos, feats, center, row_a, row_b, pair, out_a, out_b, own_feats):
    rim, channels, width = row_a.shape
    rows = center.shape[0]
    bins = feats.shape[1]
    row_start = pos[0] * rows
    odd_row = pos[0] % 2 == 1
    odd_col = pos[1] % 2 == 1
    total = rows + 2 * rim
    all_feats = feats[:channels]
    own_feats[...] = pick_bins(all_feats, row_start - rim, 1)
    col_feats = pick_bins(all_feats, pos[1] * width, 1)
    source, target = source_and_target(width, 2 * width)
    last = (target >= width) == odd_col
    copies = one_hot(source == target % 8 + jnp.where(last, width - 8, 0))
    slot = lanes((channels, width)) // 8
    for group in range(out_a.shape[0]):
        size = min(16, total - group * 16)
        blocks = []
        for k in range(size):
            e = group * 16 + k
            x = ext_row(e, odd_row, center, row_a, row_b).astype(f32)
            value = x + (col_feats + own_feats[:, e : e + 1])
            if e < rim or e >= rim + rows:
                value = value * scalar_inside(row_start - rim + e, bins)
            blocks.append(value.astype(bf16))
            pair[e] = blocks[-1]
        spread = dot(jnp.concatenate(blocks, axis=0), copies)
        for out, first in ((out_a, 0), (out_b, width)):
            parts = [
                jnp.where(
                    slot == k,
                    spread[k * channels : (k + 1) * channels, first : first + width],
                    0.0,
                )
                for k in range(size)
            ]
            while len(parts) > 1:
                parts = [sum(parts[i : i + 2]) for i in range(0, len(parts), 2)]
            out[group] = parts[0].astype(bf16)


def products(weights, taps, out, count):
    def one(row, carry):
        out[row] = dot(weights, taps[row])
        return carry

    lax.fori_loop(0, count, one, 0, unroll=4)


def combine(parts, row, spacing):
    size = parts.shape[1] // 3
    return (
        parts[row, :size]
        + parts[row + spacing, size : 2 * size]
        + parts[row + 2 * spacing, 2 * size :]
    )


def tile_kernel(
    turn, pos, weights, bias, pair, col_a, col_b, m0, m1, s1, s2, parts,
):
    total, channels, width = pair.shape
    half = width // 2
    rows, bins = pos[2], pos[4]
    rim = 6
    row_start = pos[0] * rows
    col_start = pos[1] * width
    odd_col = pos[1] % 2 == 1
    upper = 2 * row_start < bins
    first_col = half * jnp.where(upper, turn, 1 - turn) - rim
    lane = lanes((channels, width))
    slot = lane // 8
    source, target = source_and_target(2 * width, 3 * width)
    col = target % width + 2 * (target // width) + first_col
    inner = (source == col) & (source < width)
    strip = source - width
    near = strip < half
    on_left = (strip % 8 == col + 8) & (col < 0)
    on_right = (strip % 8 == col - width) & (col >= width)
    strip_ok = strip >= 0
    move = [
        one_hot(inner | (strip_ok & ((near & on_left) | (~near & on_right)))),
        one_hot(inner | (strip_ok & ((~near & on_left) | (near & on_right)))),
    ]
    for group in range(col_a.shape[0]):
        pa = col_a[group].astype(f32)
        pb = col_b[group].astype(f32)
        left = jnp.where(odd_col, pa, pb)
        right = roll(jnp.where(odd_col, pb, pa), half)
        for quad in range(4):
            blocks = []
            for k in range(4 * quad, 4 * quad + 4):
                e = 16 * group + k
                if e >= total:
                    break
                edge = jnp.where(slot == k, left, jnp.where(slot == (k + 8) % 16, right, 0.0))
                blocks.append(jnp.concatenate([pair[e], edge.astype(bf16)], axis=1))
            if not blocks:
                break
            moved = dot(jnp.concatenate(blocks, axis=0), move[quad // 2]).astype(bf16)
            for i in range(len(blocks)):
                e = 16 * group + 4 * quad + i
                for tap in range(3):
                    s1[
                        e // 2,
                        tap * channels : (tap + 1) * channels,
                        e % 2 * width : (e % 2 + 1) * width,
                    ] = moved[i * channels : (i + 1) * channels, tap * width : (tap + 1) * width]
    b1 = bias[0]
    mask1 = inside(col_start + first_col + 2, 1, bins)
    products(weights[0], s1, parts, total // 2)
    source, target = source_and_target(width, 2 * width)
    shift = one_hot(source == target % width + 4 * (target // width + 1))

    def first(c, carry):
        blocks = []
        for i in range(2):
            g = 2 * c + i
            value = jnp.maximum(combine(parts, g, 1) + b1, 0.0)
            for t in range(2):
                ok = scalar_inside(row_start - rim + 2 + 2 * g + t, bins)
                block = (value[:, t * width : (t + 1) * width] * (mask1 * ok)).astype(bf16)
                s2[g, :channels, t * width : (t + 1) * width] = block
                blocks.append(block)
        moved = dot(jnp.concatenate(blocks, axis=0), shift).astype(bf16)
        for j in range(4):
            for tap in (1, 2):
                s2[
                    2 * c + j // 2,
                    tap * channels : (tap + 1) * channels,
                    j % 2 * width : (j % 2 + 1) * width,
                ] = moved[j * channels : (j + 1) * channels, (tap - 1) * width : tap * width]
        return carry

    lax.fori_loop(0, (total - 4) // 4, first, 0, unroll=6)
    b2 = bias[1]
    products(weights[1], s2, parts, total // 2 - 2)
    low = lane < half
    quarter = m0.shape[0]
    for message, begin in (
        (m0, jnp.where(upper, 0, quarter)),
        (m1, jnp.where(upper, quarter, 0)),
    ):

        def produce(p, carry, message=message, begin=begin):
            value = jnp.maximum(combine(parts, begin + p, 2) + b2, 0.0)
            message[p] = jnp.where(low, value[:, :width], roll(value[:, width:], half)).astype(bf16)
            return carry

        lax.fori_loop(0, quarter, produce, 0, unroll=8)


def assemble_kernel(pos, m00, m01, m10, m11, coarse):
    quarter, channels, width = m00.shape
    half = width // 2
    upper = 2 * pos[0] < pos[4] // pos[2]
    low = lanes((channels, width)) < half

    def chunk(c, carry):
        u = c * 8 // quarter
        rows = []
        for i in range(8):
            p = c * 8 % quarter + i
            sides = [
                jnp.where(
                    upper, (m00, m01, m10, m11)[2 * u + v][p], (m11, m10, m01, m00)[2 * u + v][p]
                )
                for v in range(2)
            ]
            left, right = [side.astype(f32) for side in sides]
            rows.append(jnp.where(low, left, roll(right, half)).astype(bf16))
            rows.append(jnp.where(low, roll(left, half), right).astype(bf16))
        coarse[:, 16 * c : 16 * c + 16, :] = jnp.swapaxes(jnp.stack(rows, axis=0), 0, 1)
        return carry

    for c in range(quarter // 4):
        chunk(c, 0)


def strip_pack_window(pos, center, row_a, row_b, out_a, out_b):
    rim, channels, width = row_a.shape
    half = width // 2
    odd_row = pos[0] % 2 == 1
    odd_col = pos[1] % 2 == 1
    source, target = source_and_target(width, 2 * width)
    last = (target >= width) == odd_col
    spot = target % width
    copies = one_hot(
        source == spot // half * half + spot % 16 + jnp.where(last, half - 16, 0)
    )
    slot = lanes((channels, width)) % half // 16
    for group in range(out_a.shape[0]):
        block = jnp.concatenate(
            [ext_row(group * 4 + m, odd_row, center, row_a, row_b) for m in range(4)], axis=0
        )
        spread = dot(block, copies)
        for out, first in ((out_a, 0), (out_b, width)):
            parts = [spread[m * channels : (m + 1) * channels, first : first + width] for m in range(4)]
            out[group] = jnp.where(
                slot < 2,
                jnp.where(slot == 0, parts[0], parts[1]),
                jnp.where(slot == 2, parts[2], parts[3]),
            ).astype(bf16)


def fine_kernel(pos, row_weights, col_weights, bias, feats, row_terms, col_terms, terms):
    channels = bias.shape[0]
    bins = feats.shape[1]
    row_start = pos[0] * pos[2]
    col_start = pos[1] * pos[3]
    all_feats = feats[channels:]

    def stacked(start, step, shift):
        picked = pick_bins(all_feats, start, step)
        return jnp.concatenate([roll(picked, -shift * tap) for tap in range(3)], 0).astype(bf16)

    parts = dot(row_weights[...], stacked(row_start - 24, 1, 8))
    taps = [parts[e * channels : (e + 1) * channels] for e in range(3)]
    at_left = pos[1] == 0
    at = col_start - 16 + 2 * lanes((channels, 128))
    inside_taps = ((at_left) | (at < bins - 8)) & (jnp.logical_not(at_left) | (at >= 8))
    terms[0] = taps[0] + taps[1] + taps[2] + bias[...]
    terms[1] = taps[1] + jnp.where(at_left, taps[2], taps[0]) + bias[...]
    for n in range(row_terms.shape[0]):
        row_terms[n] = jnp.where(inside_taps, terms[0, :, n : n + 1], terms[1, :, n : n + 1])
    for v in range(2):
        across = dot(col_weights[...], stacked(col_start - 24 + v, 2, 4))
        for a in range(3):
            col_terms[v, a] = across[a * channels : (a + 1) * channels]


def refine_kernel(
    pos, weights, weights2, bias2, center, row_a, row_b, col_a, col_b, row_terms, col_terms,
    refined, sw, sh, products_w, products_h,
):
    pairs, channels, _ = center.shape
    rim = row_a.shape[0]
    rows, cols, bins = pos[2], pos[3], pos[4]
    row_start = pos[0] * rows
    col_start = pos[1] * cols
    odd_row = pos[0] % 2 == 1
    odd_col = pos[1] % 2 == 1
    total = pairs + 2 * rim
    slot = lanes((channels, 128)) % 64 // 16
    source, target = source_and_target(384, 768)
    tap, t = target // 128 % 3, target // 384
    col = target % 128 + 4 * tap - 12
    spot = source % 128
    same = spot // 64 == t
    place = source // 128
    move = one_hot(
        same
        & (
            ((place == 0) & (spot % 64 == col))
            | ((place == 1) & (spot % 16 == col + 16) & (col < 0))
            | ((place == 2) & (spot % 16 == col - 64) & (col >= 64))
        )
    )
    for group in range(col_a.shape[0]):
        pa, pb = col_a[group].astype(f32), col_b[group].astype(f32)
        left = jnp.where(odd_col, pa, pb)
        right = jnp.where(odd_col, pb, pa)
        blocks = []
        for m in range(4):
            x = ext_row(4 * group + m, odd_row, center, row_a, row_b)
            here = slot == m
            blocks.append(
                jnp.concatenate(
                    [x]
                    + [jnp.where(here, side, 0.0).astype(bf16) for side in (left, right)],
                    axis=1,
                )
            )
        moved = dot(jnp.concatenate(blocks, axis=0), move).astype(bf16)
        for m in range(4):
            for j in range(6):
                sw[
                    4 * group + m,
                    j % 3 * channels : (j % 3 + 1) * channels,
                    j // 3 * 128 : (j // 3 + 1) * 128,
                ] = moved[m * channels : (m + 1) * channels, j * 128 : (j + 1) * 128]
    w1 = weights[...]
    col_in = inside(col_start - 16, 2, bins)
    source, target = source_and_target(256, 384)
    spot = target % 128
    spread = one_hot(source == spot // 64 * 128 + spot % 64 + 8 * (target // 128))
    products(w1, sw, products_w, total)

    def first(n, carry):
        both = combine(products_w, n, 2)
        blocks = []
        for t in range(2):
            k = 2 * n + t
            base = both[:, t * 128 : t * 128 + 128]
            at = row_start - 16 + 2 * k
            above = scalar_inside(at - 8, bins)
            below = scalar_inside(at + 8, bins)
            mask = col_in * scalar_inside(at, bins)
            sums = [
                base + (col_terms[v, 1] + col_terms[v, 0] * above + col_terms[v, 2] * below)
                for v in range(2)
            ]
            for u in range(2):
                own = row_terms[2 * k + u]
                h = [(jnp.maximum(s + own, 0.0) * mask).astype(bf16) for s in sums]
                blocks.append(jnp.concatenate(h, axis=1))
        moved = dot(jnp.concatenate(blocks, axis=0), spread).astype(bf16)
        for j in range(4):
            for tap in range(3):
                sh[
                    2 * n + j // 2,
                    tap * channels : (tap + 1) * channels,
                    j % 2 * 128 : (j % 2 + 1) * 128,
                ] = moved[j * channels : (j + 1) * channels, tap * 128 : (tap + 1) * 128]
        return carry

    inner = total - 4
    lax.fori_loop(0, inner, first, 0, unroll=6)
    w2 = weights2[...]
    b2 = bias2[...]

    products(w2, sh, products_h, sh.shape[0])
    source, target = source_and_target(128, 128)
    weave = one_hot(2 * (source % 64) + source // 64 == target)

    def produce(c, carry):
        rows = []
        for i in range(8):
            value = jnp.maximum(combine(products_h, 8 * c + i, 8) + b2, 0.0).astype(bf16)
            both = jnp.concatenate([value[:, :128], value[:, 128:]], axis=0)
            both = dot(both, weave).astype(bf16)
            rows += [both[:channels], both[channels:]]
        at = pl.multiple_of(16 * c, 16)
        refined[:, pl.ds(at, 16), :] = jnp.swapaxes(jnp.stack(rows, axis=0), 0, 1)
        return carry

    lax.fori_loop(0, pairs // 4, produce, 0)


def per_device(
    coarse_feats, fine_feats, pair_prior, zoom_start, coarse_weights, coarse_bias,
    refine_first, refine_second, refine_bias,
):
    channels, rows, cols = pair_prior.shape
    row_count = lax.axis_size("row")
    col_count = lax.axis_size("col")
    bins = rows * row_count
    row_place = lax.axis_index("row")
    col_place = lax.axis_index("col")
    pos = jnp.stack(
        [row_place, col_place, jnp.int32(rows), jnp.int32(cols), jnp.int32(bins)]
    ).astype(jnp.int32)
    odd_row = row_place % 2 == 1
    devices = row_count * col_count

    own = jnp.concatenate([coarse_feats, fine_feats], axis=0).T
    spread = jnp.broadcast_to(own[None], (devices,) + own.shape)
    feats = lax.all_to_all(spread, ("row", "col"), split_axis=0, concat_axis=0, tiled=True)
    feats = feats.reshape(bins, 2 * channels).T

    def row_swap(block, rim):
        top, bottom = block[:rim], block[block.shape[0] - rim :]
        first, second = swap_pairs(row_count)
        return (
            lax.ppermute(jnp.where(odd_row, top, bottom), "row", first),
            lax.ppermute(jnp.where(odd_row, bottom, top), "row", second),
        )

    def col_swap(a, b):
        first, second = swap_pairs(col_count)
        return lax.ppermute(a, "col", first), lax.ppermute(b, "col", second)

    def struct(shape, dtype=bf16):
        return jax.ShapeDtypeStruct(shape, dtype)

    rim = 6
    center = jnp.transpose(pair_prior, (1, 0, 2))
    row_a, row_b = row_swap(center, rim)
    total = rows + 2 * rim
    pack = struct((pl.cdiv(total, 16), channels, 128))
    pair, *packs = call(
        pair_kernel,
        (struct((total, channels, cols)), pack, pack),
        [pltpu.VMEM((channels, 128), f32)],
        (1 << 28, 4 << 20),
        "pair",
    )(pos, feats, center, row_a, row_b)
    col_a, col_b = col_swap(*packs)
    stacked = 3 * channels

    message = struct((rows // 4, channels, 128))
    tile_weights = coarse_weights.reshape(2, stacked, stacked)
    tile_bias = coarse_bias[:, :, None]
    halves = [
        call(
            functools.partial(tile_kernel, turn),
            (message,) * 2,
            [
                pltpu.VMEM((total // 2, stacked, 256), bf16),
                pltpu.VMEM((total // 2, stacked, 256), bf16),
                pltpu.VMEM((total // 2, stacked, 256), f32),
            ],
            (3 << 30, 3 << 20),
            f"tile{turn}",
        )(
            pos, tile_weights, tile_bias, pair, col_a, col_b
        )
        for turn in range(2)
    ]
    messages = [halves[v][u] for u in range(2) for v in range(2)]
    coarse = call(
        assemble_kernel, struct((channels, rows, cols)), [], (1 << 20, 2 << 20), "assemble"
    )(pos, *messages)

    half_rows, half_cols = row_count // 2, col_count // 2
    received = [None] * 4
    for v in range(2):
        for u in range(2):
            pairs = []
            for a in range(half_rows):
                for b in range(half_cols):
                    pairs.append((a * col_count + b, (2 * a + u) * col_count + 2 * b + v))
                    pairs.append(
                        (
                            (half_rows + a) * col_count + half_cols + b,
                            (2 * a + 1 - u) * col_count + 2 * b + 1 - v,
                        )
                    )
            received[2 * u + v] = lax.ppermute(messages[2 * u + v], ("row", "col"), pairs)
    quarter = 2 * (row_place % 2) + col_place % 2
    quarter = jnp.where(zoom_start[0] > 0, 3 - quarter, quarter)
    window = jnp.where(
        quarter < 2,
        jnp.where(quarter == 0, received[0], received[1]),
        jnp.where(quarter == 2, received[2], received[3]),
    )

    parts = refine_first.reshape(3, channels, 3, 2 * channels)
    window_weights = parts[..., :channels].reshape(stacked, stacked)
    fine_parts = parts[..., channels:]
    row_terms, col_terms = call(
        fine_kernel,
        (struct((rows + 32, channels, 128), f32), struct((2, 3, channels, 128), f32)),
        [pltpu.VMEM((2, channels, 128), f32)],
        (1 << 28, 4 << 20),
        "fine",
    )(
        pos,
        fine_parts.transpose(2, 1, 0, 3).reshape(stacked, stacked),
        fine_parts.reshape(stacked, stacked),
        refine_bias[0][:, None],
        feats,
    )

    second_weights = refine_second.reshape(stacked, stacked)
    second_bias = refine_bias[1][:, None]
    window, coarse, row_terms, col_terms, window_weights, second_weights, second_bias = (
        lax.optimization_barrier(
            (window, coarse, row_terms, col_terms, window_weights, second_weights, second_bias)
        )
    )
    window_rim = 6
    row_a, row_b = row_swap(window, window_rim)
    pairs = rows // 4 + 2 * window_rim
    pack = struct((pairs // 4, channels, 128))
    col_a, col_b = col_swap(
        *call(strip_pack_window, (pack, pack), [], (1 << 20, 1 << 20), "window_strips")(
            pos, window, row_a, row_b
        )
    )
    fine_rows = rows // 2 + 16
    refined = call(
        refine_kernel,
        struct((channels, rows, cols)),
        [
            pltpu.VMEM((pairs, stacked, 256), bf16),
            pltpu.VMEM((fine_rows, stacked, 256), bf16),
            pltpu.VMEM((pairs, stacked, 256), f32),
            pltpu.VMEM((fine_rows, stacked, 256), f32),
        ],
        (3 << 30, 6 << 20),
        "refine",
    )(
        pos,
        window_weights,
        second_weights,
        second_bias,
        window, row_a, row_b, col_a, col_b, row_terms, col_terms,
    )
    return coarse, refined


def solution(mesh):
    return jax.shard_map(
        per_device,
        mesh=mesh,
        in_specs=(
            P(None, ("row", "col")),
            P(None, ("row", "col")),
            P(None, "row", "col"),
            P(),
            P(),
            P(),
            P(),
            P(),
            P(),
        ),
        out_specs=(P(None, "row", "col"), P(None, "row", "col")),
        check_vma=False,
    )
```

```python
import functools

import jax
import jax.numpy as jnp
from jax import lax
from jax.experimental import pallas as pl
from jax.experimental.pallas import tpu as pltpu
from jax.sharding import PartitionSpec as P

f32 = jnp.float32
bf16 = jnp.bfloat16
VMEM = pl.BlockSpec(memory_space=pltpu.VMEM)
SMEM = pl.BlockSpec(memory_space=pltpu.SMEM)


def call(body, outs, scratch, cost, name):
    flops, moved = cost
    def run(*args):
        return pl.pallas_call(
            body,
            out_shape=outs,
            in_specs=[SMEM] + [VMEM] * (len(args) - 1),
            out_specs=jax.tree.map(lambda _: VMEM, outs),
            scratch_shapes=scratch,
            compiler_params=pltpu.CompilerParams(vmem_limit_bytes=44 << 20),
            cost_estimate=pl.CostEstimate(flops=flops, bytes_accessed=moved, transcendentals=0),
            name=name,
        )(*args)

    return run


def roll(x, shift):
    shift = shift % x.shape[-1]
    return x if shift == 0 else pltpu.roll(x, shift, x.ndim - 1)


def lanes(shape):
    return lax.broadcasted_iota(jnp.int32, shape, len(shape) - 1)


def swap_pairs(count):
    first = [(i, i ^ 1) for i in range(count)]
    second = [(i, i + 1) for i in range(1, count - 1, 2)]
    return first, second + [(b, a) for a, b in second]


def dot(a, b):
    return jnp.dot(a, b, preferred_element_type=f32)


def one_hot(hit):
    return hit.astype(f32).astype(bf16)


def pick_at(feats, index):
    shape = (feats.shape[1], 128)
    return dot(feats, one_hot(lax.broadcasted_iota(jnp.int32, shape, 0) == index))


def pick_bins(feats, start, step):
    return pick_at(feats, start + step * lanes((1, 128)))


def source_and_target(sources, targets):
    shape = (sources, targets)
    return lax.broadcasted_iota(jnp.int32, shape, 0), lanes(shape)


def within(at, bins):
    return ((at >= 0) & (at < bins)).astype(f32)


def inside(start, step, bins, shape=(1, 128)):
    at = start + step * lanes(shape)
    return ((at >= 0) & (at < bins)).astype(f32)


def scalar_inside(at, bins):
    return ((at >= 0) & (at < bins)).astype(f32)


def ext_row(e, odd_row, center, row_a, row_b):
    rim, count = row_a.shape[0], center.shape[0]
    if e < rim:
        return jnp.where(odd_row, row_a[e], row_b[e])
    if e < rim + count:
        return center[e - rim]
    return jnp.where(odd_row, row_b[e - rim - count], row_a[e - rim - count])


def pair_kernel(pos, feats, center, row_a, row_b, pair, out_a, out_b, own_feats):
    rim, channels, width = row_a.shape
    rows = center.shape[0]
    bins = feats.shape[1]
    row_start = pos[0] * rows
    odd_row = pos[0] % 2 == 1
    odd_col = pos[1] % 2 == 1
    total = rows + 2 * rim
    all_feats = feats[:channels]
    own_feats[...] = pick_bins(all_feats, row_start - rim, 1)
    col_feats = pick_bins(all_feats, pos[1] * width, 1)
    source, target = source_and_target(width, 2 * width)
    last = (target >= width) == odd_col
    copies = one_hot(source == target % 8 + jnp.where(last, width - 8, 0))
    slot = lanes((channels, width)) // 8
    for group in range(out_a.shape[0]):
        size = min(16, total - group * 16)
        blocks = []
        for k in range(size):
            e = group * 16 + k
            x = ext_row(e, odd_row, center, row_a, row_b).astype(f32)
            value = x + (col_feats + own_feats[:, e : e + 1])
            if e < rim or e >= rim + rows:
                value = value * scalar_inside(row_start - rim + e, bins)
            blocks.append(value.astype(bf16))
            pair[e] = blocks[-1]
        spread = dot(jnp.concatenate(blocks, axis=0), copies)
        for out, first in ((out_a, 0), (out_b, width)):
            parts = [
                jnp.where(
                    slot == k,
                    spread[k * channels : (k + 1) * channels, first : first + width],
                    0.0,
                )
                for k in range(size)
            ]
            while len(parts) > 1:
                parts = [sum(parts[i : i + 2]) for i in range(0, len(parts), 2)]
            out[group] = parts[0].astype(bf16)


def products(weights, taps, out, count):
    def one(row, carry):
        out[row] = dot(weights, taps[row])
        return carry

    lax.fori_loop(0, count, one, 0, unroll=8)


def combine(parts, row, spacing):
    size = parts.shape[1] // 3
    return (
        parts[row, :size]
        + parts[row + spacing, size : 2 * size]
        + parts[row + 2 * spacing, 2 * size :]
    )


def tile_kernel(
    turn, pos, weights, bias, pair, col_a, col_b, m0, m1, s1, s2, parts,
):
    total, channels, width = pair.shape
    half = width // 2
    rows, bins = pos[2], pos[4]
    rim = 6
    row_start = pos[0] * rows
    col_start = pos[1] * width
    odd_col = pos[1] % 2 == 1
    upper = 2 * row_start < bins
    first_col = half * jnp.where(upper, turn, 1 - turn) - rim
    lane = lanes((channels, width))
    slot = lane // 8
    source, target = source_and_target(2 * width, 3 * width)
    col = target % width + 2 * (target // width) + first_col
    inner = (source == col) & (source < width)
    strip = source - width
    near = strip < half
    on_left = (strip % 8 == col + 8) & (col < 0)
    on_right = (strip % 8 == col - width) & (col >= width)
    strip_ok = strip >= 0
    move = [
        one_hot(inner | (strip_ok & ((near & on_left) | (~near & on_right)))),
        one_hot(inner | (strip_ok & ((~near & on_left) | (near & on_right)))),
    ]
    for group in range(col_a.shape[0]):
        pa = col_a[group].astype(f32)
        pb = col_b[group].astype(f32)
        left = jnp.where(odd_col, pa, pb)
        right = roll(jnp.where(odd_col, pb, pa), half)
        for quad in range(4):
            blocks = []
            for k in range(4 * quad, 4 * quad + 4):
                e = 16 * group + k
                if e >= total:
                    break
                edge = jnp.where(slot == k, left, jnp.where(slot == (k + 8) % 16, right, 0.0))
                blocks.append(jnp.concatenate([pair[e], edge.astype(bf16)], axis=1))
            if not blocks:
                break
            moved = dot(jnp.concatenate(blocks, axis=0), move[quad // 2]).astype(bf16)
            for i in range(len(blocks)):
                e = 16 * group + 4 * quad + i
                for tap in range(3):
                    s1[
                        e // 2,
                        tap * channels : (tap + 1) * channels,
                        e % 2 * width : (e % 2 + 1) * width,
                    ] = moved[i * channels : (i + 1) * channels, tap * width : (tap + 1) * width]
    b1 = bias[0]
    mask1 = inside(col_start + first_col + 2, 1, bins)
    products(weights[0], s1, parts, total // 2)
    source, target = source_and_target(width, 2 * width)
    shift = one_hot(source == target % width + 4 * (target // width + 1))

    def first(c, carry):
        blocks = []
        for i in range(2):
            g = 2 * c + i
            value = jnp.maximum(combine(parts, g, 1) + b1, 0.0)
            for t in range(2):
                ok = scalar_inside(row_start - rim + 2 + 2 * g + t, bins)
                block = (value[:, t * width : (t + 1) * width] * (mask1 * ok)).astype(bf16)
                s2[g, :channels, t * width : (t + 1) * width] = block
                blocks.append(block)
        moved = dot(jnp.concatenate(blocks, axis=0), shift).astype(bf16)
        for j in range(4):
            for tap in (1, 2):
                s2[
                    2 * c + j // 2,
                    tap * channels : (tap + 1) * channels,
                    j % 2 * width : (j % 2 + 1) * width,
                ] = moved[j * channels : (j + 1) * channels, (tap - 1) * width : tap * width]
        return carry

    lax.fori_loop(0, (total - 4) // 4, first, 0, unroll=6)
    b2 = bias[1]
    products(weights[1], s2, parts, total // 2 - 2)
    low = lane < half
    quarter = m0.shape[0]
    for message, begin in (
        (m0, jnp.where(upper, 0, quarter)),
        (m1, jnp.where(upper, quarter, 0)),
    ):

        def produce(p, carry, message=message, begin=begin):
            value = jnp.maximum(combine(parts, begin + p, 2) + b2, 0.0)
            message[p] = jnp.where(low, value[:, :width], roll(value[:, width:], half)).astype(bf16)
            return carry

        lax.fori_loop(0, quarter, produce, 0, unroll=8)


def assemble_kernel(pos, m00, m01, m10, m11, coarse):
    quarter, channels, width = m00.shape
    half = width // 2
    upper = 2 * pos[0] < pos[4] // pos[2]
    low = lanes((channels, width)) < half

    def chunk(c, carry):
        u = c * 8 // quarter
        rows = []
        for i in range(8):
            p = c * 8 % quarter + i
            sides = [
                jnp.where(
                    upper, (m00, m01, m10, m11)[2 * u + v][p], (m11, m10, m01, m00)[2 * u + v][p]
                )
                for v in range(2)
            ]
            left, right = [side.astype(f32) for side in sides]
            rows.append(jnp.where(low, left, roll(right, half)).astype(bf16))
            rows.append(jnp.where(low, roll(left, half), right).astype(bf16))
        coarse[:, 16 * c : 16 * c + 16, :] = jnp.swapaxes(jnp.stack(rows, axis=0), 0, 1)
        return carry

    for c in range(quarter // 4):
        chunk(c, 0)


def strip_pack_window(pos, center, row_a, row_b, out_a, out_b):
    rim, channels, width = row_a.shape
    half = width // 2
    odd_row = pos[0] % 2 == 1
    odd_col = pos[1] % 2 == 1
    source, target = source_and_target(width, 2 * width)
    last = (target >= width) == odd_col
    spot = target % width
    copies = one_hot(
        source == spot // half * half + spot % 16 + jnp.where(last, half - 16, 0)
    )
    slot = lanes((channels, width)) % half // 16
    for group in range(out_a.shape[0]):
        block = jnp.concatenate(
            [ext_row(group * 4 + m, odd_row, center, row_a, row_b) for m in range(4)], axis=0
        )
        spread = dot(block, copies)
        for out, first in ((out_a, 0), (out_b, width)):
            parts = [spread[m * channels : (m + 1) * channels, first : first + width] for m in range(4)]
            out[group] = jnp.where(
                slot < 2,
                jnp.where(slot == 0, parts[0], parts[1]),
                jnp.where(slot == 2, parts[2], parts[3]),
            ).astype(bf16)


def fine_kernel(pos, row_weights, col_weights, bias, feats, row_terms, col_terms, terms):
    channels = bias.shape[0]
    bins = feats.shape[1]
    row_start = pos[0] * pos[2]
    col_start = pos[1] * pos[3]
    all_feats = feats[channels:]

    def stacked(start, step, shift):
        picked = pick_bins(all_feats, start, step)
        return jnp.concatenate([roll(picked, -shift * tap) for tap in range(3)], 0).astype(bf16)

    parts = dot(row_weights[...], stacked(row_start - 24, 1, 8))
    taps = [parts[e * channels : (e + 1) * channels] for e in range(3)]
    at_left = pos[1] == 0
    at = col_start - 16 + 2 * lanes((channels, 128))
    inside_taps = ((at_left) | (at < bins - 8)) & (jnp.logical_not(at_left) | (at >= 8))
    terms[0] = taps[0] + taps[1] + taps[2] + bias[...]
    terms[1] = taps[1] + jnp.where(at_left, taps[2], taps[0]) + bias[...]
    for n in range(row_terms.shape[0]):
        row_terms[n] = jnp.where(inside_taps, terms[0, :, n : n + 1], terms[1, :, n : n + 1]).astype(bf16)
    for v in range(2):
        across = dot(col_weights[...], stacked(col_start - 24 + v, 2, 4))
        for a in range(3):
            col_terms[v, a] = across[a * channels : (a + 1) * channels]


def refine_kernel(
    pos, weights, weights2, bias2, center, row_a, row_b, col_a, col_b, row_terms, col_terms,
    refined, sw, sh, products_w, products_h,
):
    pairs, channels, _ = center.shape
    rim = row_a.shape[0]
    rows, cols, bins = pos[2], pos[3], pos[4]
    row_start = pos[0] * rows
    col_start = pos[1] * cols
    odd_row = pos[0] % 2 == 1
    odd_col = pos[1] % 2 == 1
    total = pairs + 2 * rim
    slot = lanes((channels, 128)) % 64 // 16
    source, target = source_and_target(384, 768)
    tap, t = target // 128 % 3, target // 384
    col = target % 128 + 4 * tap - 12
    spot = source % 128
    same = spot // 64 == t
    place = source // 128
    move = one_hot(
        same
        & (
            ((place == 0) & (spot % 64 == col))
            | ((place == 1) & (spot % 16 == col + 16) & (col < 0))
            | ((place == 2) & (spot % 16 == col - 64) & (col >= 64))
        )
    )
    for group in range(col_a.shape[0]):
        pa, pb = col_a[group].astype(f32), col_b[group].astype(f32)
        left = jnp.where(odd_col, pa, pb)
        right = jnp.where(odd_col, pb, pa)
        blocks = []
        for m in range(4):
            x = ext_row(4 * group + m, odd_row, center, row_a, row_b)
            here = slot == m
            blocks.append(
                jnp.concatenate(
                    [x]
                    + [jnp.where(here, side, 0.0).astype(bf16) for side in (left, right)],
                    axis=1,
                )
            )
        moved = dot(jnp.concatenate(blocks, axis=0), move).astype(bf16)
        for m in range(4):
            for j in range(6):
                sw[
                    4 * group + m,
                    j % 3 * channels : (j % 3 + 1) * channels,
                    j // 3 * 128 : (j // 3 + 1) * 128,
                ] = moved[m * channels : (m + 1) * channels, j * 128 : (j + 1) * 128]
    w1 = weights[...]
    col_in = inside(col_start - 16, 2, bins)
    source, target = source_and_target(256, 384)
    spot = target % 128
    spread = one_hot(source == spot // 64 * 128 + spot % 64 + 8 * (target // 128))
    products(w1, sw, products_w, total)

    def first(n, carry):
        both = combine(products_w, n, 2)
        blocks = []
        for t in range(2):
            k = 2 * n + t
            base = both[:, t * 128 : t * 128 + 128]
            at = row_start - 16 + 2 * k
            above = scalar_inside(at - 8, bins)
            below = scalar_inside(at + 8, bins)
            mask = col_in * scalar_inside(at, bins)
            sums = [
                base + (col_terms[v, 1] + col_terms[v, 0] * above + col_terms[v, 2] * below)
                for v in range(2)
            ]
            for u in range(2):
                own = row_terms[2 * k + u].astype(f32)
                h = [(jnp.maximum(s + own, 0.0) * mask).astype(bf16) for s in sums]
                blocks.append(jnp.concatenate(h, axis=1))
        moved = dot(jnp.concatenate(blocks, axis=0), spread).astype(bf16)
        for j in range(4):
            for tap in range(3):
                sh[
                    2 * n + j // 2,
                    tap * channels : (tap + 1) * channels,
                    j % 2 * 128 : (j % 2 + 1) * 128,
                ] = moved[j * channels : (j + 1) * channels, tap * 128 : (tap + 1) * 128]
        return carry

    inner = total - 4
    lax.fori_loop(0, inner, first, 0, unroll=6)
    w2 = weights2[...]
    b2 = bias2[...]

    products(w2, sh, products_h, sh.shape[0])
    source, target = source_and_target(128, 128)
    weave = one_hot(2 * (source % 64) + source // 64 == target)

    def produce(c, carry):
        rows = []
        for i in range(8):
            value = jnp.maximum(combine(products_h, 8 * c + i, 8) + b2, 0.0).astype(bf16)
            both = jnp.concatenate([value[:, :128], value[:, 128:]], axis=0)
            both = dot(both, weave).astype(bf16)
            rows += [both[:channels], both[channels:]]
        at = pl.multiple_of(16 * c, 16)
        refined[:, pl.ds(at, 16), :] = jnp.swapaxes(jnp.stack(rows, axis=0), 0, 1)
        return carry

    lax.fori_loop(0, pairs // 4, produce, 0)


def per_device(
    coarse_feats, fine_feats, pair_prior, zoom_start, coarse_weights, coarse_bias,
    refine_first, refine_second, refine_bias,
):
    channels, rows, cols = pair_prior.shape
    row_count = lax.axis_size("row")
    col_count = lax.axis_size("col")
    bins = rows * row_count
    row_place = lax.axis_index("row")
    col_place = lax.axis_index("col")
    pos = jnp.stack(
        [row_place, col_place, jnp.int32(rows), jnp.int32(cols), jnp.int32(bins)]
    ).astype(jnp.int32)
    odd_row = row_place % 2 == 1
    devices = row_count * col_count

    own = jnp.concatenate([coarse_feats, fine_feats], axis=0).T
    spread = jnp.broadcast_to(own[None], (devices,) + own.shape)
    feats = lax.all_to_all(spread, ("row", "col"), split_axis=0, concat_axis=0, tiled=True)
    feats = feats.reshape(bins, 2 * channels).T

    def row_swap(block, rim):
        top, bottom = block[:rim], block[block.shape[0] - rim :]
        first, second = swap_pairs(row_count)
        return (
            lax.ppermute(jnp.where(odd_row, top, bottom), "row", first),
            lax.ppermute(jnp.where(odd_row, bottom, top), "row", second),
        )

    def col_swap(a, b):
        first, second = swap_pairs(col_count)
        return lax.ppermute(a, "col", first), lax.ppermute(b, "col", second)

    def struct(shape, dtype=bf16):
        return jax.ShapeDtypeStruct(shape, dtype)

    rim = 6
    center = jnp.transpose(pair_prior, (1, 0, 2))
    row_a, row_b = row_swap(center, rim)
    total = rows + 2 * rim
    pack = struct((pl.cdiv(total, 16), channels, 128))
    pair, *packs = call(
        pair_kernel,
        (struct((total, channels, cols)), pack, pack),
        [pltpu.VMEM((channels, 128), f32)],
        (1 << 28, 4 << 20),
        "pair",
    )(pos, feats, center, row_a, row_b)
    col_a, col_b = col_swap(*packs)
    stacked = 3 * channels

    message = struct((rows // 4, channels, 128))
    tile_weights = coarse_weights.reshape(2, stacked, stacked)
    tile_bias = coarse_bias[:, :, None]
    halves = [
        call(
            functools.partial(tile_kernel, turn),
            (message,) * 2,
            [
                pltpu.VMEM((total // 2, stacked, 256), bf16),
                pltpu.VMEM((total // 2, stacked, 256), bf16),
                pltpu.VMEM((total // 2, stacked, 256), f32),
            ],
            (3 << 30, 3 << 20),
            f"tile{turn}",
        )(
            pos, tile_weights, tile_bias, pair, col_a, col_b
        )
        for turn in range(2)
    ]
    messages = [halves[v][u] for u in range(2) for v in range(2)]
    coarse = call(
        assemble_kernel, struct((channels, rows, cols)), [], (1 << 20, 2 << 20), "assemble"
    )(pos, *messages)

    half_rows, half_cols = row_count // 2, col_count // 2
    received = [None] * 4
    for v in range(2):
        for u in range(2):
            pairs = []
            for a in range(half_rows):
                for b in range(half_cols):
                    pairs.append((a * col_count + b, (2 * a + u) * col_count + 2 * b + v))
                    pairs.append(
                        (
                            (half_rows + a) * col_count + half_cols + b,
                            (2 * a + 1 - u) * col_count + 2 * b + 1 - v,
                        )
                    )
            received[2 * u + v] = lax.ppermute(messages[2 * u + v], ("row", "col"), pairs)
    quarter = 2 * (row_place % 2) + col_place % 2
    quarter = jnp.where(zoom_start[0] > 0, 3 - quarter, quarter)
    window = jnp.where(
        quarter < 2,
        jnp.where(quarter == 0, received[0], received[1]),
        jnp.where(quarter == 2, received[2], received[3]),
    )

    parts = refine_first.reshape(3, channels, 3, 2 * channels)
    window_weights = parts[..., :channels].reshape(stacked, stacked)
    fine_parts = parts[..., channels:]
    row_terms, col_terms = call(
        fine_kernel,
        (struct((rows + 32, channels, 128)), struct((2, 3, channels, 128), f32)),
        [pltpu.VMEM((2, channels, 128), f32)],
        (1 << 28, 4 << 20),
        "fine",
    )(
        pos,
        fine_parts.transpose(2, 1, 0, 3).reshape(stacked, stacked),
        fine_parts.reshape(stacked, stacked),
        refine_bias[0][:, None],
        feats,
    )

    second_weights = refine_second.reshape(stacked, stacked)
    second_bias = refine_bias[1][:, None]
    window, coarse, row_terms, col_terms, window_weights, second_weights, second_bias = (
        lax.optimization_barrier(
            (window, coarse, row_terms, col_terms, window_weights, second_weights, second_bias)
        )
    )
    window_rim = 6
    row_a, row_b = row_swap(window, window_rim)
    pairs = rows // 4 + 2 * window_rim
    pack = struct((pairs // 4, channels, 128))
    col_a, col_b = col_swap(
        *call(strip_pack_window, (pack, pack), [], (1 << 20, 1 << 20), "window_strips")(
            pos, window, row_a, row_b
        )
    )
    fine_rows = rows // 2 + 16
    refined = call(
        refine_kernel,
        struct((channels, rows, cols)),
        [
            pltpu.VMEM((pairs, stacked, 256), bf16),
            pltpu.VMEM((fine_rows, stacked, 256), bf16),
            pltpu.VMEM((pairs, stacked, 256), f32),
            pltpu.VMEM((fine_rows, stacked, 256), f32),
        ],
        (3 << 30, 6 << 20),
        "refine",
    )(
        pos,
        window_weights,
        second_weights,
        second_bias,
        window, row_a, row_b, col_a, col_b, row_terms, col_terms,
    )
    return coarse, refined


def solution(mesh):
    return jax.shard_map(
        per_device,
        mesh=mesh,
        in_specs=(
            P(None, ("row", "col")),
            P(None, ("row", "col")),
            P(None, "row", "col"),
            P(),
            P(),
            P(),
            P(),
            P(),
            P(),
        ),
        out_specs=(P(None, "row", "col"), P(None, "row", "col")),
        check_vma=False,
    )
```
